512 devices in a mesh: frame: 4 (over x), vox: 128 (over y, z, core).
Axes of the slice: x: 4, y: 8, z: 8, core: 2. Of those that a mesh axis runs over, the one named last changes fastest.
Arguments:
- volume: float32 [4, 256, 512, 128], P('frame', 'vox'), may hold values from -60 to 60
Outputs:
- factor: float32 [256, 256], replicated
The draws below stay inside these ranges and needn't reach their ends.
All inputs are finite; a program needn't handle non-finite values.
Results may differ from the reference program's by a relative error of at most 0.0001.
Values sent between devices are 32-bit elements; how exact they have to be, the bound alone decides.
No kernel may reach another device: no remote copies, remote signals or barrier semaphores. Data moves between devices by JAX's collectives and lax.ppermute only.
A program may use at most 64 MiB of HBM per device.

```python
import jax
import jax.numpy as jnp
from jax import lax

NZ = 256
XD = 4
NY = 128
FRAMES = 4
NX = 512


def draw_volume(key, part):
    full_shape = (FRAMES, NZ, NX, NY)
    key_base = jax.random.fold_in(key, 11)
    key_pair = jax.random.fold_in(key, 12)
    key_rows = jax.random.fold_in(key, 13)
    base_values = jnp.clip(jax.random.normal(key_base, full_shape, jnp.float32), -4.0, 4.0)
    num_blocks = NX // XD
    pairing = jax.vmap(lambda frame_id: jax.random.permutation(jax.random.fold_in(key_pair, frame_id), num_blocks))(jnp.arange(FRAMES))
    z_block = jnp.arange(NZ) // (NZ // num_blocks)
    x_block = jnp.arange(NX) // XD
    paired = z_block[None, :, None] == pairing[:, x_block][:, None, :]
    spike_gain = jnp.where(paired, 8.0, 1.0).astype(jnp.float32)
    values = base_values * spike_gain[:, :, :, None]
    row_scale = jnp.exp(jax.random.uniform(key_rows, (NZ,), jnp.float32, jnp.log(0.7), jnp.log(1.4)))
    values = values * row_scale[None, :, None, None]
    return values


def setup_inputs(seed: int = 0) -> dict:
    key_of = jax.random.split(jax.random.key(seed), 2)
    return {
        "volume": draw_volume(jax.random.fold_in(key_of[1], 71), 0),
    }


def reference(volume):
    rows_z = volume.shape[1]
    column_total = volume.shape[0] * volume.shape[2] * volume.shape[3]

    def add_frame(running, frame_data):
        flat = frame_data.reshape(rows_z, -1)
        return (running + jnp.dot(flat.astype(jnp.float32), flat.T.astype(jnp.float32), precision=lax.Precision.HIGHEST, preferred_element_type=jnp.float32), None)
    running, unused = lax.scan(add_frame, jnp.zeros((rows_z, rows_z), jnp.float32), volume)
    gram = running / jnp.float32(column_total)
    return jnp.linalg.cholesky(gram)
```

```python
import jax
import jax.numpy as jnp
from jax import lax
from jax.experimental import pallas as pl
from jax.experimental.pallas import tpu as pltpu
from jax.sharding import Mesh
from jax.sharding import PartitionSpec as P

VOX = ("vox_0", "vox_1", "vox_2")
PAIR = ("frame", "vox_2")


def exchange(tiles, axes):
    return lax.all_to_all(tiles, axes, split_axis=0, concat_axis=0, tiled=True)


def from_everyone(x, axes):
    return exchange(jnp.broadcast_to(x, (lax.axis_size(axes), *x.shape)), axes)


def eye_parts(half):
    rows = lax.broadcasted_iota(jnp.int32, (half, half), 0)
    cols = lax.broadcasted_iota(jnp.int32, (half, half), 1)
    return rows, cols


def folded_gram_body(scale, half, x_ref, out_ref):
    total = jnp.zeros((2 * half, 2 * half), jnp.float32)
    for line in range(x_ref.shape[1]):
        rows_z = x_ref[:, line, :]
        total += lax.dot_general(
            rows_z,
            rows_z,
            (((1,), (1,)), ((), ())),
            precision=lax.Precision.HIGHEST,
            preferred_element_type=jnp.float32,
        )
    total = total * scale
    rows, cols = eye_parts(half)
    low = total[half:, half:]
    out_ref[0:half, :] = jnp.where(rows >= cols, total[:half, :half], low)
    out_ref[half : 2 * half, :] = total[half:, :half]
    spare = out_ref.shape[0] - 2 * half
    diagonal = jnp.sum(jnp.where(rows == cols, low, 0.0), axis=0, keepdims=True)
    out_ref[2 * half :, :] = jnp.broadcast_to(diagonal, (spare, half))


def folded_gram(columns, column_total, padded):
    rows_z = columns.shape[0]
    half = rows_z // 2

    def body(x_ref, out_ref):
        folded_gram_body(1.0 / column_total, half, x_ref, out_ref)

    return pl.pallas_call(
        body,
        out_shape=jax.ShapeDtypeStruct((padded, half), jnp.float32),
        name="folded_gram",
    )(columns)


def per_device(volume):
    _, rows_z, lines, width = volume.shape
    voxes = lax.axis_size(VOX)
    half = rows_z * voxes // 2
    column_total = float(lax.axis_size("frame") * lines * width)
    tiles = volume.reshape(rows_z, voxes, lines // voxes, width).swapaxes(0, 1)
    columns = exchange(tiles, VOX).reshape(2 * half, lines // voxes, width)
    pair = lax.axis_size(PAIR)
    share = -(-(2 * half + 1) // (8 * pair)) * 8
    folded = folded_gram(columns, column_total, share * pair)
    part = jnp.sum(exchange(folded.reshape(pair, share, half), PAIR), axis=0)
    part = jnp.sum(from_everyone(part, "vox_0"), axis=0)
    part = jnp.sum(from_everyone(part, "vox_1"), axis=0)
    whole = from_everyone(part, PAIR).reshape(pair * share, half)
    rows, cols = eye_parts(half)
    top = jnp.tril(whole[:half])
    low = jnp.where(rows > cols, whole[:half].T, 0.0)
    low = low + jnp.where(rows == cols, whole[2 * half], 0.0)
    gram = jnp.concatenate(
        [
            jnp.concatenate([top, jnp.zeros_like(top)], axis=1),
            jnp.concatenate([whole[half : 2 * half], low], axis=1),
        ]
    )
    return jnp.tril(lax.linalg.cholesky(gram, symmetrize_input=False))


def solution(mesh):
    finer = Mesh(
        mesh.devices.reshape(mesh.shape["frame"], 8, 8, 2), ("frame", "vox_0", "vox_1", "vox_2")
    )
    return jax.shard_map(
        per_device,
        mesh=finer,
        in_specs=(P("frame", VOX, None, None),),
        out_specs=P(),
        check_vma=False,
    )
```

```python
import jax
import jax.numpy as jnp
from jax import lax
from jax.experimental import pallas as pl
from jax.experimental.pallas import tpu as pltpu
from jax.sharding import Mesh
from jax.sharding import PartitionSpec as P

VOX = ("vox_0", "vox_1", "vox_2")
PAIR = ("frame", "vox_2")
LANES = 128
SUBS = 8


def exchange(tiles, axes):
    return lax.all_to_all(tiles, axes, split_axis=0, concat_axis=0, tiled=True)


def from_everyone(x, axes):
    return exchange(jnp.broadcast_to(x, (lax.axis_size(axes), *x.shape)), axes)


def eye_parts(half):
    rows = lax.broadcasted_iota(jnp.int32, (half, half), 0)
    cols = lax.broadcasted_iota(jnp.int32, (half, half), 1)
    return rows, cols


def folded_gram_body(scale, half, x_ref, out_ref):
    total = jnp.zeros((2 * half, 2 * half), jnp.float32)
    for line in range(x_ref.shape[1]):
        rows_z = x_ref[:, line, :]
        total += lax.dot_general(
            rows_z,
            rows_z,
            (((1,), (1,)), ((), ())),
            precision=lax.Precision.HIGHEST,
            preferred_element_type=jnp.float32,
        )
    total = total * scale
    rows, cols = eye_parts(half)
    low = total[half:, half:]
    out_ref[0:half, :] = jnp.where(rows >= cols, total[:half, :half], low)
    out_ref[half : 2 * half, :] = total[:half, half:]
    spare = out_ref.shape[0] - 2 * half
    diagonal = jnp.sum(jnp.where(rows == cols, low, 0.0), axis=0, keepdims=True)
    out_ref[2 * half :, :] = jnp.broadcast_to(diagonal, (spare, half))


def folded_gram(columns, column_total, padded):
    rows_z = columns.shape[0]
    half = rows_z // 2

    def body(x_ref, out_ref):
        folded_gram_body(1.0 / column_total, half, x_ref, out_ref)

    return pl.pallas_call(
        body,
        out_shape=jax.ShapeDtypeStruct((padded, half), jnp.float32),
        name="folded_gram",
    )(columns)


def row_of(x, k):
    return jnp.broadcast_to(x[k : k + 1, :], x.shape)

def lane_of(x, k):
    return jnp.broadcast_to(x[:, k : k + 1], (x.shape[0], LANES))

def factor_half(work, poison):
    width = work.shape[1]
    slabs = [slice(s, s + LANES) for s in range(0, width, LANES)]
    panels = LANES // SUBS
    sub = lax.broadcasted_iota(jnp.int32, (SUBS, LANES), 0)

    def rows(i):
        return slice(i * SUBS, (i + 1) * SUBS)

    current = [work[rows(0), s] for s in slabs]
    for j in range(panels):
        here = [lane_of(current[0], j * SUBS + k) for k in range(SUBS)]
        more = j + 1 < panels
        if more:
            ahead = [work[rows(j + 1), s] for s in slabs]
            below = [lane_of(ahead[0], j * SUBS + k) for k in range(SUBS)]
        done = [jnp.zeros((SUBS, LANES), jnp.float32) for _ in slabs]
        lines = []
        for k in range(SUBS):
            inverse = lax.rsqrt(row_of(here[k], k))
            poison = poison + inverse * 0.0
            column = here[k] * inverse
            line = [row_of(c, k) * inverse for c in current]
            lines.append(line)
            if more:
                lower = below[k] * inverse
                ahead = [a - lower * y for a, y in zip(ahead, line)]
            for l in range(k + 1, SUBS):
                pick = row_of(column, l)
                here[l] = here[l] - column * pick
                if more:
                    below[l] = below[l] - lower * pick
            if k + 1 < SUBS:
                current = [c - column * y for c, y in zip(current, line)]
            done = [jnp.where(sub == k, y, d) for y, d in zip(line, done)]
        for s, d in zip(slabs, done):
            work[rows(j), s] = d
        if j + 2 < panels:
            turned = done[0].T
            for i in range(j + 2, panels):
                tile = turned[rows(i), :]
                value = [work[rows(i), s] for s in slabs]
                for k in range(SUBS):
                    factor = lane_of(tile, k)
                    value = [v - factor * y for v, y in zip(value, lines[k])]
                for s, v in zip(slabs, value):
                    work[rows(i), s] = v
        if more:
            current = ahead
    return poison

def factor_body(half, x_ref, out_ref, first, second):
    r = lax.broadcasted_iota(jnp.int32, (half, half), 0)
    c = lax.broadcasted_iota(jnp.int32, (half, half), 1)
    folded = x_ref[0:half, :]
    turned = folded.T
    first[:, 0:half] = jnp.where(r >= c, folded, turned)
    first[:, half:] = x_ref[half : 2 * half, :]
    second[...] = jnp.where(r == c, x_ref[2 * half : 2 * half + 1, :], jnp.where(r < c, folded, turned))
    poison = factor_half(first, jnp.zeros((SUBS, LANES), jnp.float32))
    across = first[:, half:]
    second[...] -= lax.dot_general(across, across, (((0,), (0,)), ((), ())), precision=lax.Precision.HIGHEST, preferred_element_type=jnp.float32)
    out_ref[0:half, half:] = jnp.zeros((half, half), jnp.float32)
    poison = factor_half(second, poison)
    spoil = poison[0:1, :]
    out_ref[half:, 0:half] = across.T + spoil
    out_ref[0:half, 0:half] = jnp.where(r >= c, first[:, 0:half].T + spoil, 0.0)
    out_ref[half:, half:] = jnp.where(r >= c, second[...].T + spoil, 0.0)

def factor(whole, half):
    return pl.pallas_call(
        lambda *refs: factor_body(half, *refs),
        out_shape=jax.ShapeDtypeStruct((2 * half, 2 * half), jnp.float32),
        scratch_shapes=[pltpu.VMEM((half, 2 * half), jnp.float32), pltpu.VMEM((half, half), jnp.float32)],
        name="factor",
    )(whole)


def per_device(volume):
    _, rows_z, lines, width = volume.shape
    voxes = lax.axis_size(VOX)
    half = rows_z * voxes // 2
    column_total = float(lax.axis_size("frame") * lines * width)
    tiles = volume.reshape(rows_z, voxes, lines // voxes, width).swapaxes(0, 1)
    columns = exchange(tiles, VOX).reshape(2 * half, lines // voxes, width)
    pair = lax.axis_size(PAIR)
    share = -(-(2 * half + 1) // (8 * pair)) * 8
    folded = folded_gram(columns, column_total, share * pair)
    part = jnp.sum(exchange(folded.reshape(pair, share, half), PAIR), axis=0)
    part = jnp.sum(from_everyone(part, "vox_0"), axis=0)
    part = jnp.sum(from_everyone(part, "vox_1"), axis=0)
    whole = from_everyone(part, PAIR).reshape(pair * share, half)
    return factor(whole, half)


def solution(mesh):
    finer = Mesh(
        mesh.devices.reshape(mesh.shape["frame"], 8, 8, 2), ("frame", "vox_0", "vox_1", "vox_2")
    )
    return jax.shard_map(
        per_device,
        mesh=finer,
        in_specs=(P("frame", VOX, None, None),),
        out_specs=P(),
        check_vma=False,
    )
```

```python
import jax
import jax.numpy as jnp
from jax import lax
from jax.experimental import pallas as pl
from jax.experimental.pallas import tpu as pltpu
from jax.sharding import Mesh
from jax.sharding import PartitionSpec as P

VOX = ("vox_0", "vox_1", "vox_2")
PAIR = ("frame", "vox_2")
LANES = 128
SUBS = 8
GROUP = 4

def row_of(x, k):
    return jnp.broadcast_to(x[k : k + 1, :], x.shape)

def lane_of(x, k):
    return jnp.broadcast_to(x[:, k : k + 1], (x.shape[0], LANES))

def crossed(a, b):
    return lax.dot_general(a, b, (((0,), (0,)), ((), ())), precision=lax.Precision.HIGHEST, preferred_element_type=jnp.float32)

def straight(a, b):
    return lax.dot_general(a, b, (((1,), (0,)), ((), ())), precision=lax.Precision.HIGHEST, preferred_element_type=jnp.float32)

def factor_half(work, poison, later=None, later_at={}):
    width = work.shape[1]
    slabs = [slice(s, s + LANES) for s in range(0, width, LANES)]
    panels = LANES // SUBS
    sub = lax.broadcasted_iota(jnp.int32, (SUBS, LANES), 0)

    def rows(i):
        return slice(i * SUBS, (i + 1) * SUBS)

    current = [work[rows(0), s] for s in slabs]
    for j in range(panels):
        here = [lane_of(current[0], j * SUBS + k) for k in range(SUBS)]
        more = j + 1 < panels
        join = (j + 1) % GROUP != 0
        if more and join:
            ahead = [work[rows(j + 1), s] for s in slabs]
            below = [lane_of(ahead[0], j * SUBS + k) for k in range(SUBS)]
        done = [jnp.zeros((SUBS, LANES), jnp.float32) for _ in slabs]
        lines = []
        for k in range(SUBS):
            inverse = lax.rsqrt(row_of(here[k], k))
            poison = poison + inverse * 0.0
            column = here[k] * inverse
            line = [row_of(c, k) * inverse for c in current]
            lines.append(line)
            if more and join:
                lower = below[k] * inverse
                ahead = [a - lower * y for a, y in zip(ahead, line)]
            for l in range(k + 1, SUBS):
                pick = row_of(column, l)
                here[l] = here[l] - column * pick
                if more and join:
                    below[l] = below[l] - lower * pick
            if k + 1 < SUBS:
                current = [c - column * y for c, y in zip(current, line)]
            done = [jnp.where(sub == k, y, d) for y, d in zip(line, done)]
        for s, d in zip(slabs, done):
            work[rows(j), s] = d
        near = GROUP * (j // GROUP) + GROUP
        if j + 2 < near:
            turned = done[0].T
            far = range(j + 2, near)
            value = {(i, n): work[rows(i), s] for i in far for n, s in enumerate(slabs)}
            for k in range(SUBS):
                for i in far:
                    factor = lane_of(turned[rows(i), :], k)
                    for n, y in enumerate(lines[k]):
                        value[i, n] = value[i, n] - factor * y
            for i in far:
                for n, s in enumerate(slabs):
                    work[rows(i), s] = value[i, n]
        if j + 1 == near and more:
            strip = work[(near - GROUP) * SUBS : near * SUBS, :]
            rest = slice(near * SUBS, LANES)
            turned = strip[:, 0:LANES].T
            for part in (slice(near * SUBS, (near + GROUP) * SUBS), slice((near + GROUP) * SUBS, LANES)):
                if part.start < LANES:
                    work[part, :] -= straight(turned[part, :], strip)
            ahead = [work[rows(j + 1), s] for s in slabs]
        if later is not None and j in later_at:
            strip = work[later_at[j] * SUBS : (j + 1) * SUBS, LANES:]
            later[...] -= crossed(strip, strip)
        if more:
            current = ahead
    return poison

def factor_body(half, x_ref, out_ref, first, second):
    r = lax.broadcasted_iota(jnp.int32, (half, half), 0)
    c = lax.broadcasted_iota(jnp.int32, (half, half), 1)
    folded = x_ref[0:half, :]
    turned = folded.T
    first[:, 0:half] = jnp.where(r >= c, folded, turned)
    first[:, half:] = x_ref[half : 2 * half, :]
    second[...] = jnp.where(r == c, x_ref[2 * half : 2 * half + 1, :], jnp.where(r < c, folded, turned))
    poison = factor_half(first, jnp.zeros((SUBS, LANES), jnp.float32), second, {7: 0, 13: 8, 15: 14})
    across = first[:, half:]
    out_ref[0:half, half:] = jnp.zeros((half, half), jnp.float32)
    poison = factor_half(second, poison)
    spoil = poison[0:1, :]
    out_ref[half:, 0:half] = across.T + spoil
    out_ref[0:half, 0:half] = jnp.where(r >= c, first[:, 0:half].T + spoil, 0.0)
    out_ref[half:, half:] = jnp.where(r >= c, second[...].T + spoil, 0.0)

def factor(whole, half):
    return pl.pallas_call(
        lambda *refs: factor_body(half, *refs),
        out_shape=jax.ShapeDtypeStruct((2 * half, 2 * half), jnp.float32),
        scratch_shapes=[pltpu.VMEM((half, 2 * half), jnp.float32), pltpu.VMEM((half, half), jnp.float32)],
        compiler_params=pltpu.CompilerParams(vmem_limit_bytes=8 << 20),
        name="factor",
    )(whole)

def exchange(tiles, axes):
    return lax.all_to_all(tiles, axes, split_axis=0, concat_axis=0, tiled=True)


def from_everyone(x, axes):
    return exchange(jnp.broadcast_to(x, (lax.axis_size(axes), *x.shape)), axes)


def folded_gram(columns, column_total, padded):
    half = columns.shape[0] // 2
    flat = columns.reshape(2 * half, -1)
    gram = jnp.dot(
        flat,
        flat.T,
        precision=lax.Precision.HIGHEST,
        preferred_element_type=jnp.float32,
    ) / jnp.float32(column_total)
    r = lax.broadcasted_iota(jnp.int32, (half, half), 0)
    c = lax.broadcasted_iota(jnp.int32, (half, half), 1)
    low = gram[half:, half:]
    diagonal = jnp.sum(jnp.where(r == c, low, 0.0), axis=0, keepdims=True)
    return jnp.concatenate(
        [
            jnp.where(r >= c, gram[:half, :half], low),
            gram[:half, half:],
            jnp.broadcast_to(diagonal, (padded - 2 * half, half)),
        ]
    )


def per_device(volume):
    _, rows_z, lines, width = volume.shape
    voxes = lax.axis_size(VOX)
    half = rows_z * voxes // 2
    column_total = float(lax.axis_size("frame") * lines * width)
    tiles = volume.reshape(rows_z, voxes, lines // voxes, width).swapaxes(0, 1)
    columns = exchange(tiles, VOX).reshape(2 * half, lines // voxes, width)
    pair = lax.axis_size(PAIR)
    share = -(-(2 * half + 1) // (8 * pair)) * 8
    folded = folded_gram(columns, column_total, share * pair)
    part = jnp.sum(exchange(folded.reshape(pair, share, half), PAIR), axis=0)
    part = jnp.sum(from_everyone(part, "vox_0"), axis=0)
    part = jnp.sum(from_everyone(part, "vox_1"), axis=0)
    whole = from_everyone(part, PAIR).reshape(pair * share, half)
    return factor(whole, half)


def solution(mesh):
    finer = Mesh(
        mesh.devices.reshape(mesh.shape["frame"], 8, 8, 2), ("frame", "vox_0", "vox_1", "vox_2")
    )
    return jax.shard_map(
        per_device,
        mesh=finer,
        in_specs=(P("frame", VOX, None, None),),
        out_specs=P(),
        check_vma=False,
    )
```

```python
import jax
import jax.numpy as jnp
from jax import lax
from jax.experimental import pallas as pl
from jax.experimental.pallas import tpu as pltpu
from jax.sharding import Mesh
from jax.sharding import PartitionSpec as P

VOX = ("vox_0", "vox_1", "vox_2")
PAIR = ("frame", "vox_2")
LANES = 128
SUBS = 8
TALL = 4
GROUP = 4

def row_of(x, k):
    return jnp.broadcast_to(x[k : k + 1, :], x.shape)

def lane_of(x, k):
    return jnp.broadcast_to(x[:, k : k + 1], (x.shape[0], LANES))

def crossed(a, b):
    return lax.dot_general(a, b, (((0,), (0,)), ((), ())), precision=lax.Precision.HIGHEST, preferred_element_type=jnp.float32)

def straight(a, b):
    return lax.dot_general(a, b, (((1,), (0,)), ((), ())), precision=lax.Precision.HIGHEST, preferred_element_type=jnp.float32)

def factor_half(work, poison, later=None, later_at={}):
    width = work.shape[1]
    slabs = [slice(s, s + LANES) for s in range(0, width, LANES)]
    panels = LANES // SUBS
    sub = lax.broadcasted_iota(jnp.int32, (SUBS, LANES), 0)

    def rows(i):
        return slice(i * SUBS, (i + 1) * SUBS)

    current = [work[rows(0), s] for s in slabs]
    for j in range(panels):
        here = [lane_of(current[0], j * SUBS + k) for k in range(SUBS)]
        more = j + 1 < panels
        join = (j + 1) % GROUP != 0
        if more and join:
            ahead = [work[rows(j + 1), s] for s in slabs]
            below = [lane_of(ahead[0], j * SUBS + k) for k in range(SUBS)]
        done = [jnp.zeros((SUBS, LANES), jnp.float32) for _ in slabs]
        lines = []
        for k in range(SUBS):
            inverse = lax.rsqrt(row_of(here[k], k))
            poison = poison + inverse * 0.0
            column = here[k] * inverse
            line = [row_of(c, k) * inverse for c in current]
            lines.append(line)
            if more and join:
                lower = below[k] * inverse
                ahead = [a - lower * y for a, y in zip(ahead, line)]
            for l in range(k + 1, SUBS):
                pick = row_of(column, l)
                here[l] = here[l] - column * pick
                if more and join:
                    below[l] = below[l] - lower * pick
            if k + 1 < SUBS:
                current = [c - column * y for c, y in zip(current, line)]
            done = [jnp.where(sub == k, y, d) for y, d in zip(line, done)]
        for s, d in zip(slabs, done):
            work[rows(j), s] = d
        near = GROUP * (j // GROUP) + GROUP
        if j + 2 < near:
            turned = done[0].T
            far = range(j + 2, near)
            value = {(i, n): work[rows(i), s] for i in far for n, s in enumerate(slabs)}
            for k in range(SUBS):
                for i in far:
                    factor = lane_of(turned[rows(i), :], k)
                    for n, y in enumerate(lines[k]):
                        value[i, n] = value[i, n] - factor * y
            for i in far:
                for n, s in enumerate(slabs):
                    work[rows(i), s] = value[i, n]
        if j + 1 == near and more:
            strip = work[(near - GROUP) * SUBS : near * SUBS, :]
            rest = slice(near * SUBS, LANES)
            turned = strip[:, 0:LANES].T
            for part in (slice(near * SUBS, (near + GROUP) * SUBS), slice((near + GROUP) * SUBS, LANES)):
                if part.start < LANES:
                    work[part, :] -= straight(turned[part, :], strip)
            ahead = [work[rows(j + 1), s] for s in slabs]
        if later is not None and j in later_at:
            strip = work[later_at[j] * SUBS : (j + 1) * SUBS, LANES:]
            later[...] -= crossed(strip, strip)
        if more:
            current = ahead
    return poison

def factor_body(half, x_ref, out_ref, first, second):
    r = lax.broadcasted_iota(jnp.int32, (half, half), 0)
    c = lax.broadcasted_iota(jnp.int32, (half, half), 1)
    folded = x_ref[0:half, :]
    turned = folded.T
    first[:, 0:half] = jnp.where(r >= c, folded, turned)
    first[:, half:] = x_ref[half : 2 * half, :]
    second[...] = jnp.where(r == c, x_ref[2 * half : 2 * half + 1, :], jnp.where(r < c, folded, turned))
    poison = factor_half(first, jnp.zeros((SUBS, LANES), jnp.float32), second, {7: 0, 13: 8, 15: 14})
    across = first[:, half:]
    out_ref[0:half, half:] = jnp.zeros((half, half), jnp.float32)
    poison = factor_half(second, poison)
    spoil = poison[0:1, :]
    out_ref[half:, 0:half] = across.T + spoil
    out_ref[0:half, 0:half] = jnp.where(r >= c, first[:, 0:half].T + spoil, 0.0)
    out_ref[half:, half:] = jnp.where(r >= c, second[...].T + spoil, 0.0)

def factor(whole, half):
    return pl.pallas_call(
        lambda *refs: factor_body(half, *refs),
        out_shape=jax.ShapeDtypeStruct((2 * half, 2 * half), jnp.float32),
        scratch_shapes=[pltpu.VMEM((half, 2 * half), jnp.float32), pltpu.VMEM((half, half), jnp.float32)],
        compiler_params=pltpu.CompilerParams(vmem_limit_bytes=8 << 20),
        name="factor",
    )(whole)

def exchange(tiles, axes):
    return lax.all_to_all(tiles, axes, split_axis=0, concat_axis=0, tiled=True)


def from_everyone(x, axes):
    return exchange(jnp.broadcast_to(x, (lax.axis_size(axes), *x.shape)), axes)


def folded_gram(columns, column_total, padded):
    half = columns.shape[0] // 2
    flat = columns.reshape(2 * half, -1)
    gram = jnp.dot(
        flat,
        flat.T,
        precision=lax.Precision.HIGHEST,
        preferred_element_type=jnp.float32,
    ) / jnp.float32(column_total)
    r = lax.broadcasted_iota(jnp.int32, (half, half), 0)
    c = lax.broadcasted_iota(jnp.int32, (half, half), 1)
    low = gram[half:, half:]
    diagonal = jnp.sum(jnp.where(r == c, low, 0.0), axis=0, keepdims=True)
    return jnp.concatenate(
        [
            jnp.where(r >= c, gram[:half, :half], low),
            gram[:half, half:],
            jnp.broadcast_to(diagonal, (padded - 2 * half, half)),
        ]
    )


def per_device(volume):
    _, rows_z, lines, width = volume.shape
    voxes = lax.axis_size(VOX)
    half = rows_z * voxes // 2
    column_total = float(lax.axis_size("frame") * lines * width)
    tiles = volume.reshape(rows_z, voxes, lines // voxes, width).swapaxes(0, 1)
    columns = exchange(tiles, VOX).reshape(2 * half, lines // voxes, width)
    pair = lax.axis_size(PAIR)
    share = -(-(2 * half + 1) // (TALL * pair)) * TALL
    folded = folded_gram(columns, column_total, share * pair)
    part = jnp.sum(exchange(folded.reshape(pair, share // TALL, TALL, half), PAIR), axis=0)
    part = jnp.sum(from_everyone(part, "vox_0"), axis=0)
    part = jnp.sum(from_everyone(part, "vox_1"), axis=0)
    whole = from_everyone(part, PAIR).reshape(pair * share, half)
    return factor(whole, half)


def solution(mesh):
    finer = Mesh(
        mesh.devices.reshape(mesh.shape["frame"], 8, 8, 2), ("frame", "vox_0", "vox_1", "vox_2")
    )
    return jax.shard_map(
        per_device,
        mesh=finer,
        in_specs=(P("frame", VOX, None, None),),
        out_specs=P(),
        check_vma=False,
    )
```

```python
import jax
import jax.numpy as jnp
from jax import lax
from jax.experimental import pallas as pl
from jax.experimental.pallas import tpu as pltpu
from jax.sharding import Mesh
from jax.sharding import PartitionSpec as P

VOX = ("vox_0", "vox_1", "vox_2")
PAIR = ("frame", "vox_2")
LANES = 128
SUBS = 8
TALL = 4
GROUP = 4

def row_of(x, k):
    return jnp.broadcast_to(x[k : k + 1, :], x.shape)

def lane_of(x, k):
    return jnp.broadcast_to(x[:, k : k + 1], (x.shape[0], LANES))

def crossed(a, b):
    return lax.dot_general(a, b, (((0,), (0,)), ((), ())), precision=lax.Precision.HIGHEST, preferred_element_type=jnp.float32)

def straight(a, b):
    return lax.dot_general(a, b, (((1,), (0,)), ((), ())), precision=lax.Precision.HIGHEST, preferred_element_type=jnp.float32)

def factor_half(work, poison, later=None, later_at={}):
    width = work.shape[1]
    slabs = [slice(s, s + LANES) for s in range(0, width, LANES)]
    panels = LANES // SUBS
    wide = GROUP * SUBS
    sub = lax.broadcasted_iota(jnp.int32, (SUBS, LANES), 0)

    def rows(i):
        return slice(i * SUBS, (i + 1) * SUBS)

    for first in range(0, panels, GROUP):
        band = [[work[rows(first + i), s] for s in slabs] for i in range(GROUP)]
        left = {}
        for m in range(wide):
            for i in range(m // SUBS, GROUP):
                left[m, i] = lane_of(band[i][0], first * SUBS + m)
        done = [[jnp.zeros((SUBS, LANES), jnp.float32) for _ in slabs] for _ in range(GROUP)]
        pivot = row_of(left[0, 0], 0)
        for m in range(wide):
            b, k = divmod(m, SUBS)
            inverse = lax.rsqrt(pivot)
            poison = poison + inverse * 0.0
            column = {i: left[m, i] * inverse for i in range(b, GROUP)}
            line = [row_of(c, k) * inverse for c in band[b]]
            if m + 1 < wide:
                b1, k1 = divmod(m + 1, SUBS)
                next_pick = row_of(left[m, b1], k1) * inverse
                pivot = row_of(left[m + 1, b1], k1) - next_pick * next_pick
            for l in range(m + 1, wide):
                bl, kl = divmod(l, SUBS)
                pick = next_pick if l == m + 1 else row_of(column[bl], kl)
                for i in range(bl, GROUP):
                    left[l, i] = left[l, i] - column[i] * pick
            done[b] = [jnp.where(sub == k, y, d) for y, d in zip(line, done[b])]
            for i in range(b if k + 1 < SUBS else b + 1, GROUP):
                band[i] = [v - column[i] * y for v, y in zip(band[i], line)]
        for i in range(GROUP):
            for s, d in zip(slabs, done[i]):
                work[rows(first + i), s] = d
        near = first + GROUP
        if near < panels:
            strip = work[first * SUBS : near * SUBS, :]
            rest = slice(near * SUBS, LANES)
            work[rest, :] -= straight(strip[:, 0:LANES].T[rest, :], strip)
        if later is not None and near in later_at:
            strip = work[later_at[near] * SUBS : near * SUBS, LANES:]
            later[...] -= crossed(strip, strip)
    return poison

def factor_body(half, x_ref, out_ref, first, second):
    r = lax.broadcasted_iota(jnp.int32, (half, half), 0)
    c = lax.broadcasted_iota(jnp.int32, (half, half), 1)
    folded = x_ref[0:half, :]
    turned = folded.T
    first[:, 0:half] = jnp.where(r >= c, folded, turned)
    first[:, half:] = x_ref[half : 2 * half, :]
    second[...] = jnp.where(r == c, x_ref[2 * half : 2 * half + 1, :], jnp.where(r < c, folded, turned))
    poison = factor_half(first, jnp.zeros((SUBS, LANES), jnp.float32), second, {8: 0, 12: 8, 16: 12})
    across = first[:, half:]
    out_ref[0:half, half:] = jnp.zeros((half, half), jnp.float32)
    poison = factor_half(second, poison)
    spoil = poison[0:1, :]
    out_ref[half:, 0:half] = across.T + spoil
    out_ref[0:half, 0:half] = jnp.where(r >= c, first[:, 0:half].T + spoil, 0.0)
    out_ref[half:, half:] = jnp.where(r >= c, second[...].T + spoil, 0.0)

def factor(whole, half):
    return pl.pallas_call(
        lambda *refs: factor_body(half, *refs),
        out_shape=jax.ShapeDtypeStruct((2 * half, 2 * half), jnp.float32),
        scratch_shapes=[pltpu.VMEM((half, 2 * half), jnp.float32), pltpu.VMEM((half, half), jnp.float32)],
        compiler_params=pltpu.CompilerParams(vmem_limit_bytes=8 << 20),
        name="factor",
    )(whole)


def exchange(tiles, axes):
    return lax.all_to_all(tiles, axes, split_axis=0, concat_axis=0, tiled=True)


def from_everyone(x, axes):
    return exchange(jnp.broadcast_to(x, (lax.axis_size(axes), *x.shape)), axes)


def folded_gram(columns, column_total, padded):
    half = columns.shape[0] // 2
    flat = columns.reshape(2 * half, -1)
    gram = jnp.dot(
        flat,
        flat.T,
        precision=lax.Precision.HIGHEST,
        preferred_element_type=jnp.float32,
    ) / jnp.float32(column_total)
    r = lax.broadcasted_iota(jnp.int32, (half, half), 0)
    c = lax.broadcasted_iota(jnp.int32, (half, half), 1)
    low = gram[half:, half:]
    diagonal = jnp.sum(jnp.where(r == c, low, 0.0), axis=0, keepdims=True)
    return jnp.concatenate(
        [
            jnp.where(r >= c, gram[:half, :half], low),
            gram[:half, half:],
            jnp.broadcast_to(diagonal, (padded - 2 * half, half)),
        ]
    )


def per_device(volume):
    _, rows_z, lines, width = volume.shape
    voxes = lax.axis_size(VOX)
    half = rows_z * voxes // 2
    column_total = float(lax.axis_size("frame") * lines * width)
    tiles = volume.reshape(rows_z, voxes, lines // voxes, width).swapaxes(0, 1)
    columns = exchange(tiles, VOX).reshape(2 * half, lines // voxes, width)
    pair = lax.axis_size(PAIR)
    share = -(-(2 * half + 1) // (TALL * pair)) * TALL
    folded = folded_gram(columns, column_total, share * pair)
    part = jnp.sum(exchange(folded.reshape(pair, share // TALL, TALL, half), PAIR), axis=0)
    part = jnp.sum(from_everyone(part, "vox_0"), axis=0)
    part = jnp.sum(from_everyone(part, "vox_1"), axis=0)
    whole = from_everyone(part, PAIR).reshape(pair * share, half)
    return factor(whole, half)


def solution(mesh):
    finer = Mesh(
        mesh.devices.reshape(mesh.shape["frame"], 8, 8, 2), ("frame", "vox_0", "vox_1", "vox_2")
    )
    return jax.shard_map(
        per_device,
        mesh=finer,
        in_specs=(P("frame", VOX, None, None),),
        out_specs=P(),
        check_vma=False,
    )
```

```python
import jax
import jax.numpy as jnp
from jax import lax
from jax.experimental import pallas as pl
from jax.experimental.pallas import tpu as pltpu
from jax.sharding import Mesh
from jax.sharding import PartitionSpec as P

VOX = ("vox_0", "vox_1", "vox_2")
PAIR = ("frame", "vox_2")
LANES = 128
SUBS = 8
TALL = 4
GROUP = 4
SPAN = 16

def row_of(x, k):
    return jnp.broadcast_to(x[k : k + 1, :], x.shape)

def lane_of(x, k):
    return jnp.broadcast_to(x[:, k : k + 1], (x.shape[0], LANES))

def pieces(x):
    high = x.astype(jnp.bfloat16)
    rest = x - high.astype(jnp.float32)
    middle = rest.astype(jnp.bfloat16)
    low = (rest - middle.astype(jnp.float32)).astype(jnp.bfloat16)
    return high, middle, low


def crossed(tall, flat, start=0):
    high, middle, low = (p.astype(jnp.float32) for p in pieces(tall))
    turned = jnp.concatenate([high, middle, low, high]).T.astype(jnp.bfloat16)
    high, middle, low = pieces(flat)
    none = jnp.zeros_like(high)
    turned = turned[start:]
    return lax.dot_general(
        jnp.concatenate([turned, turned], axis=1),
        jnp.concatenate([high, high, high, low, middle, middle, none, none]),
        (((1,), (0,)), ((), ())),
        preferred_element_type=jnp.float32,
    )


def factor_half(work, poison, later=None, later_at={}):
    width = work.shape[1]
    slabs = [slice(s, s + LANES) for s in range(0, width, LANES)]
    panels = LANES // SUBS
    wide = GROUP * SUBS
    sub = lax.broadcasted_iota(jnp.int32, (SUBS, LANES), 0)

    def rows(i):
        return slice(i * SUBS, (i + 1) * SUBS)

    for first in range(0, panels, GROUP):
        band = [[work[rows(first + i), s] for s in slabs] for i in range(GROUP)]
        done = [[jnp.zeros((SUBS, LANES), jnp.float32) for _ in slabs] for _ in range(GROUP)]
        left = {}
        for m in range(wide):
            b, k = divmod(m, SUBS)
            end = m - m % SPAN + SPAN
            if m % SPAN == 0:
                for n in range(m, end):
                    for i in range(n // SUBS, GROUP):
                        left[n, i] = lane_of(band[i][0], first * SUBS + n)
                pivot = row_of(left[m, b], k)
            inverse = lax.rsqrt(pivot)
            poison = poison + inverse * 0.0
            column = {i: left[m, i] * inverse for i in range(b, GROUP)}
            line = [row_of(c, k) * inverse for c in band[b]]
            if m + 1 < end:
                b1, k1 = divmod(m + 1, SUBS)
                next_pick = row_of(left[m, b1], k1) * inverse
                pivot = row_of(left[m + 1, b1], k1) - next_pick * next_pick
            for l in range(m + 1, end):
                bl, kl = divmod(l, SUBS)
                pick = next_pick if l == m + 1 else row_of(column[bl], kl)
                for i in range(bl, GROUP):
                    left[l, i] = left[l, i] - column[i] * pick
            done[b] = [jnp.where(sub == k, y, d) for y, d in zip(line, done[b])]
            for i in range(b if k + 1 < SUBS else b + 1, GROUP):
                band[i] = [v - column[i] * y for v, y in zip(band[i], line)]
        for i in range(GROUP):
            for s, d in zip(slabs, done[i]):
                work[rows(first + i), s] = d
        near = first + GROUP
        if near < panels:
            strip = work[first * SUBS : near * SUBS, :]
            rest = slice(near * SUBS, LANES)
            work[rest, :] -= crossed(strip[:, 0:LANES], strip, near * SUBS)
        if later is not None and near in later_at:
            strip = work[later_at[near] * SUBS : near * SUBS, LANES:]
            later[...] -= crossed(strip, strip)
    return poison

def factor_body(half, x_ref, out_ref, first, second):
    r = lax.broadcasted_iota(jnp.int32, (half, half), 0)
    c = lax.broadcasted_iota(jnp.int32, (half, half), 1)
    folded = x_ref[0:half, :]
    turned = folded.T
    first[:, 0:half] = jnp.where(r >= c, folded, turned)
    first[:, half:] = x_ref[half : 2 * half, :]
    second[...] = jnp.where(r == c, x_ref[2 * half : 2 * half + 1, :], jnp.where(r < c, folded, turned))
    poison = factor_half(first, jnp.zeros((SUBS, LANES), jnp.float32), second, {4: 0, 8: 4, 12: 8, 16: 12})
    across = first[:, half:]
    out_ref[0:half, half:] = jnp.zeros((half, half), jnp.float32)
    poison = factor_half(second, poison)
    spoil = poison[0:1, :]
    out_ref[half:, 0:half] = across.T + spoil
    out_ref[0:half, 0:half] = jnp.where(r >= c, first[:, 0:half].T + spoil, 0.0)
    out_ref[half:, half:] = jnp.where(r >= c, second[...].T + spoil, 0.0)

def factor(whole, half):
    return pl.pallas_call(
        lambda *refs: factor_body(half, *refs),
        out_shape=jax.ShapeDtypeStruct((2 * half, 2 * half), jnp.float32),
        scratch_shapes=[pltpu.VMEM((half, 2 * half), jnp.float32), pltpu.VMEM((half, half), jnp.float32)],
        compiler_params=pltpu.CompilerParams(vmem_limit_bytes=8 << 20),
        name="factor",
    )(whole)


def exchange(tiles, axes):
    return lax.all_to_all(tiles, axes, split_axis=0, concat_axis=0, tiled=True)


def from_everyone(x, axes):
    return exchange(jnp.broadcast_to(x, (lax.axis_size(axes), *x.shape)), axes)


def folded_gram(columns, column_total, padded):
    half = columns.shape[0] // 2
    flat = columns.reshape(2 * half, -1)
    gram = jnp.dot(
        flat,
        flat.T,
        precision=lax.Precision.HIGHEST,
        preferred_element_type=jnp.float32,
    ) / jnp.float32(column_total)
    r = lax.broadcasted_iota(jnp.int32, (half, half), 0)
    c = lax.broadcasted_iota(jnp.int32, (half, half), 1)
    low = gram[half:, half:]
    diagonal = jnp.sum(jnp.where(r == c, low, 0.0), axis=0, keepdims=True)
    return jnp.concatenate(
        [
            jnp.where(r >= c, gram[:half, :half], low),
            gram[:half, half:],
            jnp.broadcast_to(diagonal, (padded - 2 * half, half)),
        ]
    )


def per_device(volume):
    _, rows_z, lines, width = volume.shape
    voxes = lax.axis_size(VOX)
    half = rows_z * voxes // 2
    column_total = float(lax.axis_size("frame") * lines * width)
    tiles = volume.reshape(rows_z, voxes, lines // voxes, width).swapaxes(0, 1)
    columns = exchange(tiles, VOX).reshape(2 * half, lines // voxes, width)
    pair = lax.axis_size(PAIR)
    share = -(-(2 * half + 1) // (TALL * pair)) * TALL
    folded = folded_gram(columns, column_total, share * pair)
    part = jnp.sum(exchange(folded.reshape(pair, share // TALL, TALL, half), PAIR), axis=0)
    part = jnp.sum(from_everyone(part, "vox_0"), axis=0)
    part = jnp.sum(from_everyone(part, "vox_1"), axis=0)
    whole = from_everyone(part, PAIR).reshape(pair * share, half)
    return factor(whole, half)


def solution(mesh):
    finer = Mesh(
        mesh.devices.reshape(mesh.shape["frame"], 8, 8, 2), ("frame", "vox_0", "vox_1", "vox_2")
    )
    return jax.shard_map(
        per_device,
        mesh=finer,
        in_specs=(P("frame", VOX, None, None),),
        out_specs=P(),
        check_vma=False,
    )
```

```python
import jax
import jax.numpy as jnp
from jax import lax
from jax.experimental import pallas as pl
from jax.experimental.pallas import tpu as pltpu
from jax.sharding import Mesh
from jax.sharding import PartitionSpec as P

VOX = ("y_far", "y_near", "z_far", "z_near", "core")
NEAR = ("frame", "y_near", "z_near", "core")
FAR = ("y_far", "z_far")
LANES = 128
SUBS = 8
GROUP = 4
SPAN = 16

def row_of(x, k):
    return jnp.broadcast_to(x[k : k + 1, :], x.shape)

def lane_of(x, k):
    return jnp.broadcast_to(x[:, k : k + 1], (x.shape[0], LANES))

def pieces(x):
    high = x.astype(jnp.bfloat16)
    rest = x - high.astype(jnp.float32)
    middle = rest.astype(jnp.bfloat16)
    low = (rest - middle.astype(jnp.float32)).astype(jnp.bfloat16)
    return high, middle, low


def crossed(tall, flat, start=0):
    high, middle, low = (p.astype(jnp.float32) for p in pieces(tall))
    turned = jnp.concatenate([high, middle, low, high]).T.astype(jnp.bfloat16)
    high, middle, low = pieces(flat)
    none = jnp.zeros_like(high)
    turned = turned[start:]
    return lax.dot_general(
        jnp.concatenate([turned, turned], axis=1),
        jnp.concatenate([high, high, high, low, middle, middle, none, none]),
        (((1,), (0,)), ((), ())),
        preferred_element_type=jnp.float32,
    )


def factor_half(work, poison, later=None, later_at={}):
    width = work.shape[1]
    slabs = [slice(s, s + LANES) for s in range(0, width, LANES)]
    panels = LANES // SUBS
    wide = GROUP * SUBS
    sub = lax.broadcasted_iota(jnp.int32, (SUBS, LANES), 0)

    def rows(i):
        return slice(i * SUBS, (i + 1) * SUBS)

    for first in range(0, panels, GROUP):
        band = [[work[rows(first + i), s] for s in slabs] for i in range(GROUP)]
        done = [[jnp.zeros((SUBS, LANES), jnp.float32) for _ in slabs] for _ in range(GROUP)]
        left = {}
        for m in range(wide):
            b, k = divmod(m, SUBS)
            end = m - m % SPAN + SPAN
            if m % SPAN == 0:
                for n in range(m, end):
                    for i in range(n // SUBS, GROUP):
                        left[n, i] = lane_of(band[i][0], first * SUBS + n)
                pivot = row_of(left[m, b], k)
            inverse = lax.rsqrt(pivot)
            poison = poison + inverse * 0.0
            column = {i: left[m, i] * inverse for i in range(b, GROUP)}
            line = [row_of(c, k) * inverse for c in band[b]]
            if m + 1 < end:
                b1, k1 = divmod(m + 1, SUBS)
                next_pick = row_of(left[m, b1], k1) * inverse
                pivot = row_of(left[m + 1, b1], k1) - next_pick * next_pick
            for l in range(m + 1, end):
                bl, kl = divmod(l, SUBS)
                pick = next_pick if l == m + 1 else row_of(column[bl], kl)
                for i in range(bl, GROUP):
                    left[l, i] = left[l, i] - column[i] * pick
            done[b] = [jnp.where(sub == k, y, d) for y, d in zip(line, done[b])]
            for i in range(b if k + 1 < SUBS else b + 1, GROUP):
                band[i] = [v - column[i] * y for v, y in zip(band[i], line)]
        for i in range(GROUP):
            for s, d in zip(slabs, done[i]):
                work[rows(first + i), s] = d
        near = first + GROUP
        if near < panels:
            strip = work[first * SUBS : near * SUBS, :]
            rest = slice(near * SUBS, LANES)
            work[rest, :] -= crossed(strip[:, 0:LANES], strip, near * SUBS)
        if later is not None and near in later_at:
            strip = work[later_at[near] * SUBS : near * SUBS, LANES:]
            later[...] -= crossed(strip, strip)
    return poison

def factor_body(half, x_ref, out_ref, first, second):
    r = lax.broadcasted_iota(jnp.int32, (half, half), 0)
    c = lax.broadcasted_iota(jnp.int32, (half, half), 1)
    folded = x_ref[0:half, :]
    turned = folded.T
    first[:, 0:half] = jnp.where(r >= c, folded, turned)
    first[:, half:] = x_ref[half : 2 * half, :]
    second[...] = jnp.where(r == c, x_ref[2 * half : 2 * half + 1, :], jnp.where(r < c, folded, turned))
    poison = factor_half(first, jnp.zeros((SUBS, LANES), jnp.float32), second, {4: 0, 8: 4, 12: 8, 16: 12})
    across = first[:, half:]
    out_ref[0:half, half:] = jnp.zeros((half, half), jnp.float32)
    poison = factor_half(second, poison)
    spoil = poison[0:1, :]
    out_ref[half:, 0:half] = across.T + spoil
    out_ref[0:half, 0:half] = jnp.where(r >= c, first[:, 0:half].T + spoil, 0.0)
    out_ref[half:, half:] = jnp.where(r >= c, second[...].T + spoil, 0.0)

def factor(whole, half):
    return pl.pallas_call(
        lambda *refs: factor_body(half, *refs),
        out_shape=jax.ShapeDtypeStruct((2 * half, 2 * half), jnp.float32),
        scratch_shapes=[pltpu.VMEM((half, 2 * half), jnp.float32), pltpu.VMEM((half, half), jnp.float32)],
        compiler_params=pltpu.CompilerParams(vmem_limit_bytes=8 << 20),
        name="factor",
    )(whole)


def exchange(tiles, axes):
    return lax.all_to_all(tiles, axes, split_axis=0, concat_axis=0, tiled=True)


def summed_for(tiles, count, to):
    share = tiles.shape[0] // count

    def body(tiles_ref, out_ref):
        sums = [tiles_ref[i * share : (i + 1) * share, :] for i in range(4)]
        for i in range(4, count):
            sums[i % 4] = sums[i % 4] + tiles_ref[i * share : (i + 1) * share, :]
        total = (sums[0] + sums[1]) + (sums[2] + sums[3])
        for i in range(to):
            out_ref[i * share : (i + 1) * share, :] = total

    return pl.pallas_call(
        body,
        out_shape=jax.ShapeDtypeStruct((share * to, tiles.shape[1]), tiles.dtype),
        compiler_params=pltpu.CompilerParams(vmem_limit_bytes=4 << 20),
        name="summed_for",
    )(tiles)


def exchange_rows(rows, axes):
    count = lax.axis_size(axes)
    return exchange(rows.reshape(count, -1, 1, rows.shape[-1]), axes).reshape(rows.shape)


def folded_gram(columns, column_total, padded):
    half = columns.shape[0] // 2
    flat = columns.reshape(2 * half, -1)
    gram = jnp.dot(
        flat,
        flat.T,
        precision=lax.Precision.HIGHEST,
        preferred_element_type=jnp.float32,
    ) / jnp.float32(column_total)
    r = lax.broadcasted_iota(jnp.int32, (half, half), 0)
    c = lax.broadcasted_iota(jnp.int32, (half, half), 1)
    low = gram[half:, half:]
    diagonal = jnp.sum(jnp.where(r == c, low, 0.0), axis=0, keepdims=True)
    return jnp.concatenate(
        [
            jnp.where(r >= c, gram[:half, :half], low),
            gram[:half, half:],
            jnp.broadcast_to(diagonal, (padded - 2 * half, half)),
        ]
    )


def per_device(volume):
    _, rows_z, lines, width = volume.shape
    voxes = lax.axis_size(VOX)
    half = rows_z * voxes // 2
    column_total = float(lax.axis_size("frame") * lines * width)
    tiles = volume.reshape(rows_z, voxes, lines // voxes, width).swapaxes(0, 1)
    columns = exchange(tiles, VOX).reshape(2 * half, lines // voxes, width)
    near, far = lax.axis_size(NEAR), lax.axis_size(FAR)
    share = -(-(2 * half + 1) // near)
    folded = folded_gram(columns, column_total, share * near)
    part = summed_for(exchange_rows(folded, NEAR), near, far)
    part = summed_for(exchange_rows(part, FAR), far, near)
    whole = exchange_rows(part, NEAR)
    return factor(whole, half)


def solution(mesh):
    finer = Mesh(
        mesh.devices.reshape(mesh.shape["frame"], 4, 2, 4, 2, 2), ("frame", *VOX)
    )
    return jax.shard_map(
        per_device,
        mesh=finer,
        in_specs=(P("frame", VOX, None, None),),
        out_specs=P(),
        check_vma=False,
    )
```

```python
import jax
import jax.numpy as jnp
from jax import lax
from jax.experimental import pallas as pl
from jax.experimental.pallas import tpu as pltpu
from jax.sharding import Mesh
from jax.sharding import PartitionSpec as P

VOX = ("y_far", "y_near", "z_far", "z_near", "core")
NEAR = ("frame", "y_near", "z_near", "core")
FAR = ("y_far", "z_far")
LANES = 128
SUBS = 8
GROUP = 4
SPAN = 16

def row_of(x, k):
    return jnp.broadcast_to(x[k : k + 1, :], x.shape)

def lane_of(x, k):
    return jnp.broadcast_to(x[:, k : k + 1], (x.shape[0], LANES))

def pieces(x):
    high = x.astype(jnp.bfloat16)
    rest = x - high.astype(jnp.float32)
    middle = rest.astype(jnp.bfloat16)
    low = (rest - middle.astype(jnp.float32)).astype(jnp.bfloat16)
    return high, middle, low


def crossed(tall, flat, start=0):
    high, middle, low = (p.astype(jnp.float32) for p in pieces(tall))
    turned = jnp.concatenate([high, middle, low, high]).T.astype(jnp.bfloat16)
    high, middle, low = pieces(flat)
    none = jnp.zeros_like(high)
    turned = turned[start:]
    return lax.dot_general(
        jnp.concatenate([turned, turned], axis=1),
        jnp.concatenate([high, high, high, low, middle, middle, none, none]),
        (((1,), (0,)), ((), ())),
        preferred_element_type=jnp.float32,
    )


def factor_half(work, poison, later=None, later_at={}):
    width = work.shape[1]
    slabs = [slice(s, s + LANES) for s in range(0, width, LANES)]
    panels = LANES // SUBS
    wide = GROUP * SUBS
    sub = lax.broadcasted_iota(jnp.int32, (SUBS, LANES), 0)

    def rows(i):
        return slice(i * SUBS, (i + 1) * SUBS)

    for first in range(0, panels, GROUP):
        band = [[work[rows(first + i), s] for s in slabs] for i in range(GROUP)]
        done = [[jnp.zeros((SUBS, LANES), jnp.float32) for _ in slabs] for _ in range(GROUP)]
        left = {}
        for m in range(wide):
            b, k = divmod(m, SUBS)
            end = m - m % SPAN + SPAN
            if m % SPAN == 0:
                for n in range(m, end):
                    for i in range(n // SUBS, GROUP):
                        left[n, i] = lane_of(band[i][0], first * SUBS + n)
                pivot = row_of(left[m, b], k)
            inverse = lax.rsqrt(pivot)
            poison = poison + inverse * 0.0
            column = {i: left[m, i] * inverse for i in range(b, GROUP)}
            line = [row_of(c, k) * inverse for c in band[b]]
            if m + 1 < end:
                b1, k1 = divmod(m + 1, SUBS)
                next_pick = row_of(left[m, b1], k1) * inverse
                pivot = row_of(left[m + 1, b1], k1) - next_pick * next_pick
            for l in range(m + 1, end):
                bl, kl = divmod(l, SUBS)
                pick = next_pick if l == m + 1 else row_of(column[bl], kl)
                for i in range(bl, GROUP):
                    left[l, i] = left[l, i] - column[i] * pick
            done[b] = [jnp.where(sub == k, y, d) for y, d in zip(line, done[b])]
            for i in range(b if k + 1 < SUBS else b + 1, GROUP):
                band[i] = [v - column[i] * y for v, y in zip(band[i], line)]
        for i in range(GROUP):
            for s, d in zip(slabs, done[i]):
                work[rows(first + i), s] = d
        near = first + GROUP
        if near < panels:
            strip = work[first * SUBS : near * SUBS, :]
            rest = slice(near * SUBS, LANES)
            work[rest, :] -= crossed(strip[:, 0:LANES], strip, near * SUBS)
        if later is not None and near in later_at:
            strip = work[later_at[near] * SUBS : near * SUBS, LANES:]
            later[...] -= crossed(strip, strip)
    return poison

def factor_body(half, x_ref, out_ref, first, second):
    r = lax.broadcasted_iota(jnp.int32, (half, half), 0)
    c = lax.broadcasted_iota(jnp.int32, (half, half), 1)
    folded = x_ref[0:half, :]
    turned = folded.T
    first[:, 0:half] = jnp.where(r >= c, folded, turned)
    first[:, half:] = x_ref[half : 2 * half, :]
    second[...] = jnp.where(r == c, x_ref[2 * half : 2 * half + 1, :], jnp.where(r < c, folded, turned))
    poison = factor_half(first, jnp.zeros((SUBS, LANES), jnp.float32), second, {4: 0, 8: 4, 12: 8, 16: 12})
    across = first[:, half:]
    out_ref[0:half, half:] = jnp.zeros((half, half), jnp.float32)
    poison = factor_half(second, poison)
    spoil = poison[0:1, :]
    out_ref[half:, 0:half] = across.T + spoil
    out_ref[0:half, 0:half] = jnp.where(r >= c, first[:, 0:half].T + spoil, 0.0)
    out_ref[half:, half:] = jnp.where(r >= c, second[...].T + spoil, 0.0)

def factor(whole, half):
    return pl.pallas_call(
        lambda *refs: factor_body(half, *refs),
        out_shape=jax.ShapeDtypeStruct((2 * half, 2 * half), jnp.float32),
        scratch_shapes=[pltpu.VMEM((half, 2 * half), jnp.float32), pltpu.VMEM((half, half), jnp.float32)],
        compiler_params=pltpu.CompilerParams(vmem_limit_bytes=8 << 20),
        name="factor",
    )(whole)


def exchange(tiles, axes):
    return lax.all_to_all(tiles, axes, split_axis=0, concat_axis=0, tiled=True)


def summed_for(tiles, count, to):
    share = tiles.shape[0] // count

    def body(tiles_ref, out_ref):
        sums = [tiles_ref[i * share : (i + 1) * share, :] for i in range(4)]
        for i in range(4, count):
            sums[i % 4] = sums[i % 4] + tiles_ref[i * share : (i + 1) * share, :]
        total = (sums[0] + sums[1]) + (sums[2] + sums[3])
        for i in range(to):
            out_ref[i * share : (i + 1) * share, :] = total

    return pl.pallas_call(
        body,
        out_shape=jax.ShapeDtypeStruct((share * to, tiles.shape[1]), tiles.dtype),
        compiler_params=pltpu.CompilerParams(vmem_limit_bytes=4 << 20),
        name="summed_for",
    )(tiles)


def exchange_rows(rows, axes):
    count = lax.axis_size(axes)
    return exchange(rows.reshape(count, -1, 1, rows.shape[-1]), axes).reshape(rows.shape)


def folded_gram(columns, column_total, padded):
    half = columns.shape[0] // 2
    flat = columns.reshape(2 * half, -1)
    gram = jnp.dot(
        flat,
        flat.T,
        precision=lax.Precision.HIGHEST,
        preferred_element_type=jnp.float32,
    ) / jnp.float32(column_total)
    r = lax.broadcasted_iota(jnp.int32, (half, half), 0)
    c = lax.broadcasted_iota(jnp.int32, (half, half), 1)
    low = gram[half:, half:]
    diagonal = jnp.sum(jnp.where(r == c, low, 0.0), axis=0, keepdims=True)
    return jnp.concatenate(
        [
            jnp.where(r >= c, gram[:half, :half], low),
            gram[:half, half:],
            jnp.broadcast_to(diagonal, (padded - 2 * half, half)),
        ]
    )


def by_receiver(volume, voxes):
    _, rows_z, lines, width = volume.shape
    tiles = volume.reshape(rows_z, voxes, lines // voxes, width)

    def body(*refs):
        from_refs, to_ref, sems = refs[:rows_z], refs[rows_z], refs[rows_z + 1]
        copies = [
            pltpu.make_async_copy(from_ref, to_ref.at[:, z], sems.at[z])
            for z, from_ref in enumerate(from_refs)
        ]
        for copy in copies:
            copy.start()
        for copy in copies:
            copy.wait()

    return pl.pallas_call(
        body,
        out_shape=jax.ShapeDtypeStruct((voxes, rows_z, lines // voxes, width), volume.dtype),
        in_specs=[pl.BlockSpec(memory_space=pl.ANY)] * rows_z,
        out_specs=pl.BlockSpec(memory_space=pltpu.VMEM),
        scratch_shapes=[pltpu.SemaphoreType.DMA((rows_z,))],
        compiler_params=pltpu.CompilerParams(vmem_limit_bytes=4 << 20),
        name="by_receiver",
    )(*(tiles[z] for z in range(rows_z)))


def per_device(volume):
    _, rows_z, lines, width = volume.shape
    voxes = lax.axis_size(VOX)
    half = rows_z * voxes // 2
    column_total = float(lax.axis_size("frame") * lines * width)
    columns = exchange(by_receiver(volume, voxes), VOX).reshape(2 * half, lines // voxes, width)
    near, far = lax.axis_size(NEAR), lax.axis_size(FAR)
    share = -(-(2 * half + 1) // near)
    folded = folded_gram(columns, column_total, share * near)
    part = summed_for(exchange_rows(folded, NEAR), near, far)
    part = summed_for(exchange_rows(part, FAR), far, near)
    whole = exchange_rows(part, NEAR)
    return factor(whole, half)


def solution(mesh):
    finer = Mesh(
        mesh.devices.reshape(mesh.shape["frame"], 4, 2, 4, 2, 2), ("frame", *VOX)
    )
    return jax.shard_map(
        per_device,
        mesh=finer,
        in_specs=(P("frame", VOX, None, None),),
        out_specs=P(),
        check_vma=False,
    )
```

```python
import jax
import jax.numpy as jnp
from jax import lax
from jax.experimental import pallas as pl
from jax.experimental.pallas import tpu as pltpu
from jax.sharding import Mesh
from jax.sharding import PartitionSpec as P

VOX = ("y_far", "y_near", "z_far", "z_near", "core")
NEAR = ("frame", "y_near", "z_near", "core")
FAR = ("y_far", "z_far")
LANES = 128
SUBS = 8
GROUP = 4
SPAN = 16

def row_of(x, k):
    return jnp.broadcast_to(x[k : k + 1, :], x.shape)

def lane_of(x, k):
    return jnp.broadcast_to(x[:, k : k + 1], (x.shape[0], LANES))

def pieces(x):
    high = x.astype(jnp.bfloat16)
    rest = x - high.astype(jnp.float32)
    middle = rest.astype(jnp.bfloat16)
    low = (rest - middle.astype(jnp.float32)).astype(jnp.bfloat16)
    return high, middle, low


def crossed(tall, flat, start=0):
    high, middle, low = (p.astype(jnp.float32) for p in pieces(tall))
    turned = jnp.concatenate([high, middle, low, high]).T.astype(jnp.bfloat16)
    high, middle, low = pieces(flat)
    none = jnp.zeros_like(high)
    turned = turned[start:]
    return lax.dot_general(
        jnp.concatenate([turned, turned], axis=1),
        jnp.concatenate([high, high, high, low, middle, middle, none, none]),
        (((1,), (0,)), ((), ())),
        preferred_element_type=jnp.float32,
    )


def factor_half(work, poison, later=None, later_at={}):
    width = work.shape[1]
    slabs = [slice(s, s + LANES) for s in range(0, width, LANES)]
    panels = LANES // SUBS
    wide = GROUP * SUBS
    sub = lax.broadcasted_iota(jnp.int32, (SUBS, LANES), 0)

    def rows(i):
        return slice(i * SUBS, (i + 1) * SUBS)

    for first in range(0, panels, GROUP):
        band = [[work[rows(first + i), s] for s in slabs] for i in range(GROUP)]
        done = [[jnp.zeros((SUBS, LANES), jnp.float32) for _ in slabs] for _ in range(GROUP)]
        left = {}
        for m in range(wide):
            b, k = divmod(m, SUBS)
            end = m - m % SPAN + SPAN
            if m % SPAN == 0:
                for n in range(m, end):
                    for i in range(n // SUBS, GROUP):
                        left[n, i] = lane_of(band[i][0], first * SUBS + n)
                pivot = row_of(left[m, b], k)
            inverse = lax.rsqrt(pivot)
            poison = poison + inverse * 0.0
            column = {i: left[m, i] * inverse for i in range(b, GROUP)}
            line = [row_of(c, k) * inverse for c in band[b]]
            if m + 1 < end:
                b1, k1 = divmod(m + 1, SUBS)
                next_pick = row_of(left[m, b1], k1) * inverse
                pivot = row_of(left[m + 1, b1], k1) - next_pick * next_pick
            for l in range(m + 1, end):
                bl, kl = divmod(l, SUBS)
                pick = next_pick if l == m + 1 else row_of(column[bl], kl)
                for i in range(bl, GROUP):
                    left[l, i] = left[l, i] - column[i] * pick
            done[b] = [jnp.where(sub == k, y, d) for y, d in zip(line, done[b])]
            for i in range(b if k + 1 < SUBS else b + 1, GROUP):
                band[i] = [v - column[i] * y for v, y in zip(band[i], line)]
        for i in range(GROUP):
            for s, d in zip(slabs, done[i]):
                work[rows(first + i), s] = d
        near = first + GROUP
        if near < panels:
            strip = work[first * SUBS : near * SUBS, :]
            rest = slice(near * SUBS, LANES)
            work[rest, :] -= crossed(strip[:, 0:LANES], strip, near * SUBS)
        if later is not None and near in later_at:
            strip = work[later_at[near] * SUBS : near * SUBS, LANES:]
            later[...] -= crossed(strip, strip)
    return poison

def factor_body(half, x_ref, out_ref, first, second, full, sems):
    r = lax.broadcasted_iota(jnp.int32, (half, half), 0)
    c = lax.broadcasted_iota(jnp.int32, (half, half), 1)
    folded = x_ref[0:half, :]
    turned = folded.T
    first[:, 0:half] = jnp.where(r >= c, folded, turned)
    first[:, half:] = x_ref[half : 2 * half, :]
    second[...] = jnp.where(r == c, x_ref[2 * half : 2 * half + 1, :], jnp.where(r < c, folded, turned))
    poison = factor_half(first, jnp.zeros((SUBS, LANES), jnp.float32), second, {4: 0, 8: 4, 12: 8, 16: 12})
    top, left, corner = (
        pltpu.make_async_copy(full.at[rows, cols], out_ref.at[rows, cols], sems.at[i])
        for i, (rows, cols) in enumerate(
            (
                (slice(0, half), slice(0, 2 * half)),
                (slice(half, 2 * half), slice(0, half)),
                (slice(half, 2 * half), slice(half, 2 * half)),
            )
        )
    )
    full[0:half, half:] = jnp.zeros((half, half), jnp.float32)
    full[0:half, 0:half] = jnp.where(r >= c, first[:, 0:half].T, 0.0)
    top.start()
    full[half:, 0:half] = first[:, half:].T
    left.start()
    poison = factor_half(second, poison)
    full[half:, half:] = jnp.where(r >= c, second[...].T, 0.0)
    corner.start()
    top.wait()
    left.wait()
    corner.wait()

    @pl.when(jnp.logical_not(poison[0, 0] == 0.0))
    def _():
        spoil = poison[0:1, :]
        full[0:half, 0:half] = jnp.where(r >= c, spoil, 0.0)
        full[half:, 0:half] = jnp.broadcast_to(spoil, (half, half))
        full[half:, half:] = jnp.where(r >= c, spoil, 0.0)
        for copy in (top, left, corner):
            copy.start()
        for copy in (top, left, corner):
            copy.wait()


def factor(whole, half):
    return pl.pallas_call(
        lambda *refs: factor_body(half, *refs),
        out_shape=jax.ShapeDtypeStruct((2 * half, 2 * half), jnp.float32),
        out_specs=pl.BlockSpec(memory_space=pl.ANY),
        scratch_shapes=[
            pltpu.VMEM((half, 2 * half), jnp.float32),
            pltpu.VMEM((half, half), jnp.float32),
            pltpu.VMEM((2 * half, 2 * half), jnp.float32),
            pltpu.SemaphoreType.DMA((3,)),
        ],
        compiler_params=pltpu.CompilerParams(vmem_limit_bytes=8 << 20),
        name="factor",
    )(whole)


def exchange(tiles, axes):
    return lax.all_to_all(tiles, axes, split_axis=0, concat_axis=0, tiled=True)


def summed_for(tiles, count, to):
    share = tiles.shape[0] // count

    def body(tiles_ref, out_ref):
        sums = [tiles_ref[i * share : (i + 1) * share, :] for i in range(4)]
        for i in range(4, count):
            sums[i % 4] = sums[i % 4] + tiles_ref[i * share : (i + 1) * share, :]
        total = (sums[0] + sums[1]) + (sums[2] + sums[3])
        for i in range(to):
            out_ref[i * share : (i + 1) * share, :] = total

    return pl.pallas_call(
        body,
        out_shape=jax.ShapeDtypeStruct((share * to, tiles.shape[1]), tiles.dtype),
        compiler_params=pltpu.CompilerParams(vmem_limit_bytes=4 << 20),
        name="summed_for",
    )(tiles)


def exchange_rows(rows, axes):
    count = lax.axis_size(axes)
    return exchange(rows.reshape(count, -1, 1, rows.shape[-1]), axes).reshape(rows.shape)


def folded_gram(columns, column_total, padded):
    half = columns.shape[0] // 2
    flat = columns.reshape(2 * half, -1)
    gram = jnp.dot(
        flat,
        flat.T,
        precision=lax.Precision.HIGHEST,
        preferred_element_type=jnp.float32,
    ) / jnp.float32(column_total)
    r = lax.broadcasted_iota(jnp.int32, (half, half), 0)
    c = lax.broadcasted_iota(jnp.int32, (half, half), 1)
    low = gram[half:, half:]
    diagonal = jnp.sum(jnp.where(r == c, low, 0.0), axis=0, keepdims=True)
    return jnp.concatenate(
        [
            jnp.where(r >= c, gram[:half, :half], low),
            gram[:half, half:],
            jnp.broadcast_to(diagonal, (padded - 2 * half, half)),
        ]
    )


def by_receiver(volume, voxes):
    _, rows_z, lines, width = volume.shape
    tiles = volume.reshape(rows_z, voxes, lines // voxes, width)

    def body(*refs):
        from_refs, to_ref, sems = refs[:rows_z], refs[rows_z], refs[rows_z + 1]
        copies = [
            pltpu.make_async_copy(from_ref, to_ref.at[:, z], sems.at[z])
            for z, from_ref in enumerate(from_refs)
        ]
        for copy in copies:
            copy.start()
        for copy in copies:
            copy.wait()

    return pl.pallas_call(
        body,
        out_shape=jax.ShapeDtypeStruct((voxes, rows_z, lines // voxes, width), volume.dtype),
        in_specs=[pl.BlockSpec(memory_space=pl.ANY)] * rows_z,
        out_specs=pl.BlockSpec(memory_space=pltpu.VMEM),
        scratch_shapes=[pltpu.SemaphoreType.DMA((rows_z,))],
        compiler_params=pltpu.CompilerParams(vmem_limit_bytes=4 << 20),
        name="by_receiver",
    )(*(tiles[z] for z in range(rows_z)))


def per_device(volume):
    _, rows_z, lines, width = volume.shape
    voxes = lax.axis_size(VOX)
    half = rows_z * voxes // 2
    column_total = float(lax.axis_size("frame") * lines * width)
    columns = exchange(by_receiver(volume, voxes), VOX).reshape(2 * half, lines // voxes, width)
    near, far = lax.axis_size(NEAR), lax.axis_size(FAR)
    share = -(-(2 * half + 1) // near)
    folded = folded_gram(columns, column_total, share * near)
    part = summed_for(exchange_rows(folded, NEAR), near, far)
    part = summed_for(exchange_rows(part, FAR), far, near)
    whole = exchange_rows(part, NEAR)
    return factor(whole, half)


def solution(mesh):
    finer = Mesh(
        mesh.devices.reshape(mesh.shape["frame"], 4, 2, 4, 2, 2), ("frame", *VOX)
    )
    return jax.shard_map(
        per_device,
        mesh=finer,
        in_specs=(P("frame", VOX, None, None),),
        out_specs=P(),
        check_vma=False,
    )
```

```python
import jax
import jax.numpy as jnp
from jax import lax
from jax.experimental import pallas as pl
from jax.experimental.pallas import tpu as pltpu
from jax.sharding import Mesh
from jax.sharding import PartitionSpec as P

VOX = ("y_far", "y_near", "z_far", "z_near", "core")
NEAR = ("frame", "y_near", "z_near", "core")
FAR = ("y_far", "z_far")
LANES = 128
SUBS = 8
GROUP = 4
SPAN = 16

def row_of(x, k):
    return jnp.broadcast_to(x[k : k + 1, :], x.shape)

def lane_of(x, k):
    return jnp.broadcast_to(x[:, k : k + 1], (x.shape[0], LANES))

def pieces(x):
    high = x.astype(jnp.bfloat16)
    rest = x - high.astype(jnp.float32)
    middle = rest.astype(jnp.bfloat16)
    low = (rest - middle.astype(jnp.float32)).astype(jnp.bfloat16)
    return high, middle, low


def crossed(tall, flat, start=0):
    high, middle, low = (p.astype(jnp.float32) for p in pieces(tall))
    turned = jnp.concatenate([high, middle, low, high]).T.astype(jnp.bfloat16)
    high, middle, low = pieces(flat)
    none = jnp.zeros_like(high)
    turned = turned[start:]
    return lax.dot_general(
        jnp.concatenate([turned, turned], axis=1),
        jnp.concatenate([high, high, high, low, middle, middle, none, none]),
        (((1,), (0,)), ((), ())),
        preferred_element_type=jnp.float32,
    )


def factor_half(work, poison, later=None, later_at={}):
    width = work.shape[1]
    slabs = [slice(s, s + LANES) for s in range(0, width, LANES)]
    panels = LANES // SUBS
    wide = GROUP * SUBS
    sub = lax.broadcasted_iota(jnp.int32, (SUBS, LANES), 0)

    def rows(i):
        return slice(i * SUBS, (i + 1) * SUBS)

    for first in range(0, panels, GROUP):
        band = [[work[rows(first + i), s] for s in slabs] for i in range(GROUP)]
        done = [[jnp.zeros((SUBS, LANES), jnp.float32) for _ in slabs] for _ in range(GROUP)]
        left = {}
        for m in range(wide):
            b, k = divmod(m, SUBS)
            end = m - m % SPAN + SPAN
            if m % SPAN == 0:
                for n in range(m, end):
                    for i in range(n // SUBS, GROUP):
                        left[n, i] = lane_of(band[i][0], first * SUBS + n)
                pivot = row_of(left[m, b], k)
            inverse = lax.rsqrt(pivot)
            column = {i: left[m, i] * inverse for i in range(b, GROUP)}
            line = [row_of(c, k) * inverse for c in band[b]]
            if m + 1 < end:
                b1, k1 = divmod(m + 1, SUBS)
                next_pick = row_of(left[m, b1], k1) * inverse
                pivot = row_of(left[m + 1, b1], k1) - next_pick * next_pick
            for l in range(m + 1, end):
                bl, kl = divmod(l, SUBS)
                pick = next_pick if l == m + 1 else row_of(column[bl], kl)
                for i in range(bl, GROUP):
                    left[l, i] = left[l, i] - column[i] * pick
            done[b] = [jnp.where(sub == k, y, d) for y, d in zip(line, done[b])]
            for i in range(b if k + 1 < SUBS else b + 1, GROUP):
                band[i] = [v - column[i] * y for v, y in zip(band[i], line)]
        for i in range(GROUP):
            for s, d in zip(slabs, done[i]):
                work[rows(first + i), s] = d
        near = first + GROUP
        if near < panels:
            strip = work[first * SUBS : near * SUBS, :]
            rest = slice(near * SUBS, LANES)
            work[rest, :] -= crossed(strip[:, 0:LANES], strip, near * SUBS)
        if later is not None and near in later_at:
            strip = work[later_at[near] * SUBS : near * SUBS, LANES:]
            later[...] -= crossed(strip, strip)
    return poison + inverse * 0.0

def factor_body(half, x_ref, out_ref, first, second):
    r = lax.broadcasted_iota(jnp.int32, (half, half), 0)
    c = lax.broadcasted_iota(jnp.int32, (half, half), 1)
    folded = x_ref[0:half, :]
    turned = folded.T
    first[:, 0:half] = jnp.where(r >= c, folded, turned)
    first[:, half:] = x_ref[half : 2 * half, :]
    second[...] = jnp.where(r == c, x_ref[2 * half : 2 * half + 1, :], jnp.where(r < c, folded, turned))
    poison = factor_half(first, jnp.zeros((SUBS, LANES), jnp.float32), second, {4: 0, 8: 4, 12: 8, 16: 12})
    across = first[:, half:]
    out_ref[0:half, half:] = jnp.zeros((half, half), jnp.float32)
    poison = factor_half(second, poison)
    spoil = poison[0:1, :]
    out_ref[half:, 0:half] = across.T + spoil
    out_ref[0:half, 0:half] = jnp.where(r >= c, first[:, 0:half].T + spoil, 0.0)
    out_ref[half:, half:] = jnp.where(r >= c, second[...].T + spoil, 0.0)

def factor(whole, half):
    return pl.pallas_call(
        lambda *refs: factor_body(half, *refs),
        out_shape=jax.ShapeDtypeStruct((2 * half, 2 * half), jnp.float32),
        scratch_shapes=[pltpu.VMEM((half, 2 * half), jnp.float32), pltpu.VMEM((half, half), jnp.float32)],
        compiler_params=pltpu.CompilerParams(vmem_limit_bytes=8 << 20),
        name="factor",
    )(whole)


def exchange(tiles, axes):
    return lax.all_to_all(tiles, axes, split_axis=0, concat_axis=0, tiled=True)


def summed_for(tiles, count, to):
    share = tiles.shape[0] // count

    def body(tiles_ref, out_ref):
        sums = [tiles_ref[i * share : (i + 1) * share, :] for i in range(4)]
        for i in range(4, count):
            sums[i % 4] = sums[i % 4] + tiles_ref[i * share : (i + 1) * share, :]
        total = (sums[0] + sums[1]) + (sums[2] + sums[3])
        for i in range(to):
            out_ref[i * share : (i + 1) * share, :] = total

    return pl.pallas_call(
        body,
        out_shape=jax.ShapeDtypeStruct((share * to, tiles.shape[1]), tiles.dtype),
        compiler_params=pltpu.CompilerParams(vmem_limit_bytes=4 << 20),
        name="summed_for",
    )(tiles)


def exchange_rows(rows, axes):
    count = lax.axis_size(axes)
    return exchange(rows.reshape(count, -1, 1, rows.shape[-1]), axes).reshape(rows.shape)


def folded_gram(columns, column_total, padded):
    half = columns.shape[0] // 2
    flat = columns.reshape(2 * half, -1)
    gram = jnp.dot(
        flat,
        flat.T,
        precision=lax.Precision.HIGHEST,
        preferred_element_type=jnp.float32,
    ) / jnp.float32(column_total)
    r = lax.broadcasted_iota(jnp.int32, (half, half), 0)
    c = lax.broadcasted_iota(jnp.int32, (half, half), 1)
    low = gram[half:, half:]
    diagonal = jnp.sum(jnp.where(r == c, low, 0.0), axis=0, keepdims=True)
    return jnp.concatenate(
        [
            jnp.where(r >= c, gram[:half, :half], low),
            gram[:half, half:],
            jnp.broadcast_to(diagonal, (padded - 2 * half, half)),
        ]
    )


def by_receiver(volume, voxes):
    _, rows_z, lines, width = volume.shape
    tiles = volume.reshape(rows_z, voxes, lines // voxes, width)

    def body(*refs):
        from_refs, to_ref, sems = refs[:rows_z], refs[rows_z], refs[rows_z + 1]
        copies = [
            pltpu.make_async_copy(from_ref, to_ref.at[:, z], sems.at[z])
            for z, from_ref in enumerate(from_refs)
        ]
        for copy in copies:
            copy.start()
        for copy in copies:
            copy.wait()

    return pl.pallas_call(
        body,
        out_shape=jax.ShapeDtypeStruct((voxes, rows_z, lines // voxes, width), volume.dtype),
        in_specs=[pl.BlockSpec(memory_space=pl.ANY)] * rows_z,
        out_specs=pl.BlockSpec(memory_space=pltpu.VMEM),
        scratch_shapes=[pltpu.SemaphoreType.DMA((rows_z,))],
        compiler_params=pltpu.CompilerParams(vmem_limit_bytes=4 << 20),
        name="by_receiver",
    )(*(tiles[z] for z in range(rows_z)))


def per_device(volume):
    _, rows_z, lines, width = volume.shape
    voxes = lax.axis_size(VOX)
    half = rows_z * voxes // 2
    column_total = float(lax.axis_size("frame") * lines * width)
    columns = exchange(by_receiver(volume, voxes), VOX).reshape(2 * half, lines // voxes, width)
    near, far = lax.axis_size(NEAR), lax.axis_size(FAR)
    share = -(-(2 * half + 1) // near)
    folded = folded_gram(columns, column_total, share * near)
    part = summed_for(exchange_rows(folded, NEAR), near, far)
    part = summed_for(exchange_rows(part, FAR), far, near)
    whole = exchange_rows(part, NEAR)
    return factor(whole, half)


def solution(mesh):
    finer = Mesh(
        mesh.devices.reshape(mesh.shape["frame"], 4, 2, 4, 2, 2), ("frame", *VOX)
    )
    return jax.shard_map(
        per_device,
        mesh=finer,
        in_specs=(P("frame", VOX, None, None),),
        out_specs=P(),
        check_vma=False,
    )
```
